32 devices in a mesh: row: 16 (over z, y, x), col: 2 (over core).
Axes of the slice: x: 2, y: 2, z: 4, core: 2. Of those that a mesh axis runs over, the one named last changes fastest.
Arguments:
- tokens: bfloat16 [8192, 6144], P('row', 'col'), may hold values from -6 to 6
- w_blocks: bfloat16 [96, 81920], P('col', 'row'), may hold values from -0.25 to 0.25
- hidden_bias: bfloat16 [12288], P('col'), may hold values from -3 to 3
- pattern: int32 [96, 5], replicated, may hold values from 0 to 47, as said below
- grad_act: bfloat16 [8192, 12288], P('row', 'col'), may hold values from -6 to 6
Outputs:
- activation: bfloat16 [8192, 12288], P('row', 'col')
- weight_grad: float32 [96, 81920], P('col', 'row')
- bias_grad: float32 [12288], P('col')
The draws below stay inside these ranges and needn't reach their ends.
Inputs may be any that keep to these rules, and one draw needn't show every extreme that they name: `pattern`: panel p holds input blocks p * 24 to (p + 1) * 24 - 1, and hidden block h lies in group g = h // 48. Slot 0 of h names a block in panel g; slot k for 1 <= k <= 3 names a block in panel (g + 2^(k-1)) mod 2; slot 4 names one of the blocks 0 to 1. Names may repeat within a hidden block.
All inputs are finite; a program needn't handle non-finite values.
Results may differ from the reference program's by a relative error of at most 0.003.
Values may be sent and summed in bfloat16 or wider, within the bound.
A program may use at most 192 MiB of HBM per device.

```python
import math
import jax
import jax.numpy as jnp
from jax import lax

D = 6144
FF = 12288
BLK = 128
LEVELS = 3
GLOB = 2
KSLOT = 5
DB = 48
HB = 96
GROUPS = 2
PANEL = 24
HBC = 48
TOKENS = 8192


def draw_pattern(key, part):
    hidden_ids = jnp.arange(HB, dtype=jnp.int32)
    group_ids = hidden_ids // HBC
    subkeys = jax.random.split(key, LEVELS + 2)
    columns = []
    for slot_index in range(LEVELS + 1):
        offset = 0 if slot_index == 0 else 2 ** (slot_index - 1)
        home_panel = (group_ids + offset) % GROUPS
        picks = jax.random.randint(subkeys[slot_index], (HB,), 0, PANEL, dtype=jnp.int32)
        columns.append(home_panel * PANEL + picks)
    columns.append(jax.random.randint(subkeys[LEVELS + 1], (HB,), 0, GLOB, dtype=jnp.int32))
    pattern = jnp.stack(columns, axis=1)
    pattern = pattern.at[HB - 1, 0].set(DB - 1)
    return pattern


def steps_of(key, extent, cuts, least, largest):
    loudness = 1.0
    for axis_at, parts in cuts:
        draws = jax.random.uniform(jax.random.fold_in(jax.random.fold_in(key, 6), axis_at), (parts,), jnp.float32, least / len(cuts), largest / len(cuts))
        loudness = loudness * jnp.repeat(jnp.exp(draws), extent[axis_at] // parts).reshape((-1,) + (1,) * (len(extent) - 1 - axis_at))
    return loudness


def scatter_about(stream_key, dims, deviation, reach, cuts=(), kind=jnp.bfloat16):
    level = steps_of(stream_key, dims, cuts, -0.22, 0.18) if cuts else 1.0
    values = jax.random.normal(stream_key, dims, jnp.float32) * deviation * level
    return jnp.minimum(jnp.maximum(values, -reach), reach).astype(kind)


def setup_inputs(seed: int = 0) -> dict:
    key_list = jax.random.split(jax.random.key(seed), 6)
    return {
        "tokens": scatter_about(key_list[0], (TOKENS, D), 1.0, 6.0, ((0, 16), (1, 2))),
        "w_blocks": scatter_about(key_list[1], (HB, KSLOT * BLK * BLK), (KSLOT * BLK) ** -0.5, 0.25, ((0, 2), (1, 16))),
        "hidden_bias": scatter_about(key_list[2], (FF,), 0.5, 3.0, ((0, 2),)),
        "pattern": draw_pattern(jax.random.fold_in(key_list[5], 71), 0),
        "grad_act": scatter_about(key_list[4], (TOKENS, FF), 1.0, 6.0, ((0, 16), (1, 2))),
    }


def reference(tokens, w_blocks, hidden_bias, pattern, grad_act):
    tok_count = tokens.shape[0]
    tok_blocks = tokens.reshape(tok_count, DB, BLK)
    inv_scale = 1.0 / math.sqrt(tok_count)

    def per_block(block_index):
        slot_ids = pattern[block_index]
        selected = jnp.take(tok_blocks, slot_ids, axis=1).reshape(tok_count, KSLOT * BLK).astype(jnp.float32)
        block_weight = w_blocks[block_index].reshape(KSLOT * BLK, BLK).astype(jnp.float32)
        bias_piece = lax.dynamic_slice_in_dim(hidden_bias, block_index * BLK, BLK).astype(jnp.float32)
        pre_act = jnp.dot(selected, block_weight, preferred_element_type=jnp.float32) + bias_piece
        act_value, pull_back = jax.vjp(jax.nn.gelu, pre_act)
        grad_piece = lax.dynamic_slice_in_dim(grad_act, block_index * BLK, BLK, 1).astype(jnp.float32)
        grad_pre = pull_back(grad_piece)[0]
        grad_rounded = lax.optimization_barrier(grad_pre.astype(jnp.bfloat16)).astype(jnp.float32)
        weight_piece = jnp.dot(selected.T, grad_rounded, preferred_element_type=jnp.float32) * inv_scale
        bias_piece_grad = lax.optimization_barrier(jnp.sum(grad_pre, axis=0)) * inv_scale
        return (act_value.astype(jnp.bfloat16), weight_piece.reshape(-1), bias_piece_grad)
    acts, weight_grad, bias_parts = lax.map(per_block, jnp.arange(HB, dtype=jnp.int32))
    activation = jnp.transpose(acts, (1, 0, 2)).reshape(tok_count, HB * BLK)
    return (activation, weight_grad, bias_parts.reshape(HB * BLK))
```

```python
import functools
import math

import jax
import jax.numpy as jnp
from jax import lax
from jax.experimental import pallas as pl
from jax.experimental.pallas import tpu as pltpu
from jax.sharding import PartitionSpec as P

BLK = 128
LEVELS = 3
GLOB = 2
KSLOT = 5
MESH = pl.DeviceIdType.MESH
VMEM_LIMIT = 60 * 1024 * 1024


def from_behind(block, axis, distance):
    devices = range(lax.axis_size(axis))
    route = [((i - distance) % len(devices), i) for i in devices]
    return lax.ppermute(block, axis, route)


def broadcast(value, axis, source):
    kept = jnp.where(lax.axis_index(axis) == source, value, 0).astype(value.dtype)
    return lax.psum(kept, axis)


def plain_body(tokens, w_blocks, hidden_bias, pattern, grad_act):
    tok_rows = tokens.shape[0]
    local_blocks = w_blocks.shape[0]
    col_count = lax.axis_size("col")
    col_index = lax.axis_index("col")
    panel_blocks = tokens.shape[1] // BLK
    inv_scale = 1.0 / math.sqrt(tok_rows * lax.axis_size("row"))
    gathered_weights = lax.all_gather(w_blocks, "row", axis=1, tiled=True)
    weights = gathered_weights.reshape(local_blocks, KSLOT, BLK, BLK)
    my_pattern = lax.dynamic_slice_in_dim(pattern, col_index * local_blocks, local_blocks, 0)
    own_panel = tokens.reshape(tok_rows, panel_blocks, BLK)
    pieces = [jnp.take(own_panel, my_pattern[:, 0] - col_index * panel_blocks, axis=1)]
    for level_index in range(LEVELS):
        offset = 2**level_index % col_count
        if offset == 0:
            source = own_panel
        else:
            moved = from_behind(tokens, "col", -offset)
            source = moved.reshape(tok_rows, panel_blocks, BLK)
        home_panel = (col_index + offset) % col_count
        pieces.append(
            jnp.take(source, my_pattern[:, level_index + 1] - home_panel * panel_blocks, axis=1)
        )
    shared = broadcast(tokens[:, : GLOB * BLK], "col", 0).reshape(tok_rows, GLOB, BLK)
    pieces.append(jnp.take(shared, my_pattern[:, LEVELS + 1], axis=1))
    picked = jnp.stack(pieces, axis=2)
    pre_act = jnp.einsum("thkc,hkcd->thd", picked, weights, preferred_element_type=jnp.float32)
    pre_act = pre_act + hidden_bias.astype(jnp.float32).reshape(local_blocks, BLK)
    act_value, pull_back = jax.vjp(jax.nn.gelu, pre_act)
    activation = act_value.reshape(tok_rows, local_blocks * BLK).astype(jnp.bfloat16)
    grad_pre = pull_back(grad_act.astype(jnp.float32).reshape(tok_rows, local_blocks, BLK))[0]
    grad_rounded = grad_pre.astype(jnp.bfloat16)
    weight_terms = (
        jnp.einsum("thkc,thd->hkcd", picked, grad_rounded, preferred_element_type=jnp.float32)
        * inv_scale
    )
    weight_terms = weight_terms.reshape(local_blocks, KSLOT * BLK * BLK)
    weight_grad = lax.psum_scatter(weight_terms, "row", scatter_dimension=1, tiled=True)
    bias_terms = jnp.sum(grad_pre, axis=0).reshape(local_blocks * BLK) * inv_scale
    bias_grad = lax.psum(bias_terms, "row")
    return (activation, weight_grad, bias_grad)


def place(quads):
    row = lax.axis_index("row")
    return row, row // 4, (row // 2) % 2, row % 2, lax.axis_index("col")


def greet(row, quad, bit_y, bit_x, col, quads, extra=()):
    barrier = pltpu.get_barrier_semaphore()
    peers = [(quad * 4 + bit_y * 2 + 1 - bit_x, col), (quad * 4 + (1 - bit_y) * 2 + bit_x, col)]
    peers += [((quad + d) % quads * 4 + bit_y * 2 + bit_x, col) for d in range(1, quads)]
    peers += list(extra)
    for peer in peers:
        pl.semaphore_signal(barrier, inc=1, device_id=peer, device_id_type=MESH)
    pl.semaphore_wait(barrier, len(peers))


def gather_kernel(quads, w_ref, tok_ref, all_ref, peer_ref,
                  own_sem, tok_s, tok_r, z_s, z_r, y_s, y_r, x_s, x_r):
    row, quad, bit_y, bit_x, col = place(quads)
    half = w_ref.shape[0] // 2
    x_peer = (quad * 4 + bit_y * 2 + 1 - bit_x, col)
    y_peer = (quad * 4 + (1 - bit_y) * 2 + bit_x, col)
    greet(row, quad, bit_y, bit_x, col, quads, [(row, 1 - col)])

    def send(src, dst, s, r, peer):
        copy = pltpu.make_async_remote_copy(
            src_ref=src, dst_ref=dst, send_sem=s, recv_sem=r, device_id=peer, device_id_type=MESH
        )
        copy.start()
        return copy

    copies = []
    own = pltpu.make_async_copy(w_ref, all_ref.at[row], own_sem)
    own.start()
    z_copies = []
    for d in range(1, quads):
        target = ((quad + d) % quads * 4 + bit_y * 2 + bit_x, col)
        z_copies.append(send(w_ref, all_ref.at[row], z_s.at[d - 1], z_r.at[d - 1], target))
    cut = [pl.ds(0, half), pl.ds(half, half)]
    first_y, first_x = [], []
    for d in range(quads):
        src_row = (quad - d + quads) % quads * 4 + bit_y * 2 + bit_x
        if d > 0:
            z_copies[d - 1].wait_recv()
        src = [w_ref.at[c] if d == 0 else all_ref.at[src_row, c] for c in cut]
        dst = [all_ref.at[src_row, c] for c in cut]
        first_y.append(send(src[0], dst[0], y_s.at[d], y_r.at[d], y_peer))
        first_x.append(send(src[1], dst[1], x_s.at[d], x_r.at[d], x_peer))
        copies.append(send(src[0], dst[0], x_s.at[quads + d], x_r.at[quads + d], x_peer))
        copies.append(send(src[1], dst[1], y_s.at[quads + d], y_r.at[quads + d], y_peer))
        if d == 0:
            tok_copy = send(tok_ref, peer_ref, tok_s, tok_r, (row, 1 - col))
    for d in range(quads):
        from_quad = (quad - d + quads) % quads * 4
        y_row = from_quad + (1 - bit_y) * 2 + bit_x
        x_row = from_quad + bit_y * 2 + 1 - bit_x
        first_y[d].wait_recv()
        piece = all_ref.at[y_row, cut[0]]
        copies.append(send(piece, piece, x_s.at[2 * quads + d], x_r.at[2 * quads + d], x_peer))
        first_x[d].wait_recv()
        piece = all_ref.at[x_row, cut[1]]
        copies.append(send(piece, piece, y_s.at[2 * quads + d], y_r.at[2 * quads + d], y_peer))
    for copy in copies:
        copy.wait()
    for copy in z_copies + first_y + first_x:
        copy.wait_send()
    tok_copy.wait()
    own.wait()


def gather(w_flat, tokens, quads):
    any_spec = pl.BlockSpec(memory_space=pl.ANY)
    dma = pltpu.SemaphoreType.DMA
    return pl.pallas_call(
        functools.partial(gather_kernel, quads),
        out_shape=(
            jax.ShapeDtypeStruct((quads * 4,) + w_flat.shape, w_flat.dtype),
            jax.ShapeDtypeStruct(tokens.shape, tokens.dtype),
        ),
        in_specs=[pl.BlockSpec(memory_space=pltpu.VMEM), any_spec],
        out_specs=(any_spec, any_spec),
        scratch_shapes=[dma, dma, dma, dma((quads - 1,)), dma((quads - 1,)),
                        dma((3 * quads,)), dma((3 * quads,)), dma((3 * quads,)), dma((3 * quads,))],
        compiler_params=pltpu.CompilerParams(collective_id=0, has_side_effects=True,
                                             vmem_limit_bytes=VMEM_LIMIT),
    )(w_flat, tokens)


def compute_kernel(rows, pairs_rows, scale, offsets, pat_ref, own_ref, peer_ref, shared_ref,
                   w_ref, bias_ref, grad_ref, act_ref, part_ref, bgrad_ref):
    step = pl.program_id(0)
    weights = [w_ref[r].astype(jnp.float32) for r in range(rows)]
    results = []
    for j in range(2):
        piece = pl.ds(j * BLK, BLK)
        w = jnp.concatenate([v[j * pairs_rows:(j + 1) * pairs_rows] for v in weights], axis=0)
        w = w.astype(jnp.bfloat16)
        base = (2 * step + j) * KSLOT
        picks = []
        for k in range(KSLOT):
            source = own_ref
            if k == KSLOT - 1:
                source = shared_ref
            elif k > 0 and offsets[k - 1]:
                source = peer_ref
            at = pl.multiple_of(pat_ref[base + k] * BLK, BLK)
            picks.append(source[:, pl.ds(at, BLK)])
        sel = jnp.concatenate(picks, axis=1)
        v = jnp.dot(sel, w, preferred_element_type=jnp.float32)
        v = v + bias_ref[:, piece].astype(jnp.float32)
        c = math.sqrt(2.0 / math.pi)
        sq = v * v
        t = jnp.tanh(v * (c + (c * 0.044715) * sq))
        lift = 0.5 + 0.5 * t
        act_ref[:, piece] = (v * lift).astype(jnp.bfloat16)
        slope = lift + (0.5 * v) * (1.0 - t * t) * (c + (3.0 * 0.044715 * c) * sq)
        grad = grad_ref[:, piece].astype(jnp.float32) * slope
        bgrad_ref[:, piece] = jnp.sum(grad, axis=0, keepdims=True) * scale
        out = lax.dot_general(sel, grad.astype(jnp.bfloat16), (((0,), (0,)), ((), ())),
                              preferred_element_type=jnp.float32)
        results.append(out * scale)
    for r in range(rows):
        cut = slice(r * pairs_rows, (r + 1) * pairs_rows)
        part_ref[r] = jnp.concatenate([o[cut] for o in results], axis=0).astype(part_ref.dtype)


def compute(pat, own, peer, shared, weights, bias, grad_act, rows, offsets, scale):
    tok = own.shape[0]
    hidden = grad_act.shape[1]
    steps = hidden // (2 * BLK)
    piece = weights.shape[1] // (2 * steps)
    whole = lambda a: pl.BlockSpec(a.shape, lambda i, p: (0, 0))
    wide = lambda n: pl.BlockSpec((n, 2 * BLK), lambda i, p: (0, i))
    cube = pl.BlockSpec((rows, 2 * piece, BLK), lambda i, p: (0, i, 0))
    return pl.pallas_call(
        functools.partial(compute_kernel, rows, piece, scale, offsets),
        out_shape=(
            jax.ShapeDtypeStruct((tok, hidden), jnp.bfloat16),
            jax.ShapeDtypeStruct(weights.shape, jnp.bfloat16),
            jax.ShapeDtypeStruct((1, hidden), jnp.float32),
        ),
        grid_spec=pltpu.PrefetchScalarGridSpec(
            num_scalar_prefetch=1, grid=(steps,),
            in_specs=[whole(own), whole(peer), whole(shared), cube, wide(1), wide(tok)],
            out_specs=[wide(tok), cube, wide(1)],
        ),
        compiler_params=pltpu.CompilerParams(vmem_limit_bytes=VMEM_LIMIT),
    )(pat, own, peer, shared, weights, bias, grad_act)


def scatter_kernel(quads, chunk, p_ref, b_ref, out_ref, bout_ref,
                   first, second, second_out, third, third_out,
                   bx, by, by_out, bz, bz_out,
                   f_s, f_r, s_s, s_r, t_s, t_r, b_s, b_r):
    row, quad, bit_y, bit_x, col = place(quads)
    half = p_ref.shape[1] // 2
    x_peer = (quad * 4 + bit_y * 2 + 1 - bit_x, col)
    y_peer = (quad * 4 + (1 - bit_y) * 2 + bit_x, col)
    peers = [x_peer, y_peer]
    greet(row, quad, bit_y, bit_x, col, quads)

    def send(src, dst, s, r, peer):
        copy = pltpu.make_async_remote_copy(
            src_ref=src, dst_ref=dst, send_sem=s, recv_sem=r, device_id=peer, device_id_type=MESH
        )
        copy.start()
        return copy

    def piece_row(quad_at, colour, near, far):
        flip_x, flip_y = (near, far) if colour == 0 else (far, near)
        x = (1 - bit_x) if flip_x else bit_x
        y = (1 - bit_y) if flip_y else bit_y
        return quad_at * 4 + y * 2 + x

    order = list(range(1, quads)) + [0]
    bias_copies = [send(b_ref, bx, b_s.at[0], b_r.at[0], x_peer)]
    firsts = {}
    for far in (1, 0):
        for d in order:
            at = (quad + d) % quads
            for colour in range(2):
                firsts[colour, far, d] = send(
                    p_ref.at[piece_row(at, colour, 1, far), pl.ds(colour * half, half)],
                    first.at[colour, far, d], f_s.at[colour, far, d], f_r.at[colour, far, d],
                    peers[colour])
    bias_copies[0].wait()
    by_out[...] = b_ref[...] + bx[...]
    bias_copies.append(send(by_out, by, b_s.at[1], b_r.at[1], y_peer))
    seconds = {}
    for d in order:
        at = (quad + d) % quads
        for colour in range(2):
            firsts[colour, 1, d].wait_recv()
            mine = piece_row(at, colour, 0, 1)

            @pl.loop(0, half // chunk)
            def _(i, colour=colour, d=d, mine=mine):
                s = pl.multiple_of(i * chunk, chunk)
                here = p_ref[mine, pl.ds(colour * half + s, chunk), :].astype(jnp.float32)
                come = first[colour, 1, d, pl.ds(s, chunk), :].astype(jnp.float32)
                second_out[colour, d, pl.ds(s, chunk), :] = (here + come).astype(jnp.bfloat16)

            seconds[colour, d] = send(second_out.at[colour, d], second.at[colour, d],
                                      s_s.at[colour, d], s_r.at[colour, d], peers[1 - colour])
    bias_copies[1].wait()
    bz_out[...] = by_out[...] + by[...]
    for d in range(1, quads):
        target = ((quad + d) % quads * 4 + bit_y * 2 + bit_x, col)
        bias_copies.append(send(bz_out, bz.at[d - 1], b_s.at[d + 1], b_r.at[d + 1], target))
    thirds = []
    for d in order:
        at = (quad + d) % quads
        for colour in range(2):
            firsts[colour, 0, d].wait_recv()
            seconds[colour, d].wait_recv()
            mine = piece_row(at, colour, 0, 0)

            @pl.loop(0, half // chunk)
            def _(i, colour=colour, d=d, mine=mine):
                s = pl.multiple_of(i * chunk, chunk)
                total = p_ref[mine, pl.ds(colour * half + s, chunk), :].astype(jnp.float32)
                total += first[colour, 0, d, pl.ds(s, chunk), :].astype(jnp.float32)
                total += second[colour, d, pl.ds(s, chunk), :].astype(jnp.float32)
                if d == 0:
                    out_ref[pl.ds(colour * half + s, chunk), :] = total
                else:
                    third_out[colour, d - 1, pl.ds(s, chunk), :] = total.astype(jnp.bfloat16)

            if d > 0:
                target = (at * 4 + bit_y * 2 + bit_x, col)
                thirds.append(send(third_out.at[colour, d - 1], third.at[colour, d - 1],
                                   t_s.at[colour, d - 1], t_r.at[colour, d - 1], target))
    for copy in bias_copies[2:]:
        copy.wait()
    total = bz_out[...]
    for d in range(quads - 1):
        total += bz[d]
    bout_ref[...] = total
    for copy in thirds:
        copy.wait()
    for colour in range(2):
        @pl.loop(0, half // chunk)
        def _(i, colour=colour):
            s = pl.multiple_of(i * chunk, chunk)
            total = out_ref[pl.ds(colour * half + s, chunk), :]
            for d in range(quads - 1):
                total += third[colour, d, pl.ds(s, chunk), :].astype(jnp.float32)
            out_ref[pl.ds(colour * half + s, chunk), :] = total
    for copy in list(firsts.values()) + list(seconds.values()):
        copy.wait_send()


def scatter(parts, bias_terms, quads):
    n = parts.shape[1]
    half = n // 2
    chunk = next(c for c in (192, 160, 128, 96, 80, 64, 48, 32, 16) if half % c == 0)
    vmem = pl.BlockSpec(memory_space=pltpu.VMEM)
    dma = pltpu.SemaphoreType.DMA
    bf = lambda *s: pltpu.VMEM(s, jnp.bfloat16)
    f32 = lambda *s: pltpu.VMEM(s, jnp.float32)
    b = bias_terms.shape
    return pl.pallas_call(
        functools.partial(scatter_kernel, quads, chunk),
        out_shape=(jax.ShapeDtypeStruct((n, BLK), jnp.float32),
                   jax.ShapeDtypeStruct(b, jnp.float32)),
        in_specs=[vmem, vmem],
        out_specs=(vmem, vmem),
        scratch_shapes=[
            bf(2, 2, quads, half, BLK), bf(2, quads, half, BLK), bf(2, quads, half, BLK),
            bf(2, quads - 1, half, BLK), bf(2, quads - 1, half, BLK),
            f32(*b), f32(*b), f32(*b), f32(quads - 1, *b), f32(*b),
            dma((2, 2, quads)), dma((2, 2, quads)), dma((2, quads)), dma((2, quads)),
            dma((2, quads - 1)), dma((2, quads - 1)), dma((quads + 1,)), dma((quads + 1,)),
        ],
        compiler_params=pltpu.CompilerParams(collective_id=1, has_side_effects=True,
                                             vmem_limit_bytes=VMEM_LIMIT),
    )(parts, bias_terms)


def kernel_body(tokens, w_blocks, hidden_bias, pattern, grad_act):
    tok_rows = tokens.shape[0]
    local_blocks, width = w_blocks.shape
    rows = lax.axis_size("row")
    quads = rows // 4
    col_count = lax.axis_size("col")
    col = lax.axis_index("col")
    panel_blocks = tokens.shape[1] // BLK
    scale = 1.0 / math.sqrt(tok_rows * rows)
    offsets = [2**level % col_count for level in range(LEVELS)]
    mine = lax.dynamic_slice_in_dim(pattern, col * local_blocks, local_blocks, 0)
    homes = [(col + o) % col_count * panel_blocks for o in [0] + offsets] + [0]
    pat = (mine - jnp.stack([jnp.asarray(h, jnp.int32) for h in homes])).reshape(-1)
    flat = w_blocks.reshape(local_blocks * width // BLK, BLK)
    weights, peer = gather(flat, tokens, quads)
    shared = jnp.where(col == 0, tokens[:, : GLOB * BLK], peer[:, : GLOB * BLK])
    activation, parts, bias_terms = compute(
        pat, tokens, peer, shared, weights, hidden_bias.reshape(1, -1), grad_act,
        rows, offsets, scale)
    weight_grad, bias_grad = scatter(parts, bias_terms.reshape(-1, BLK), quads)
    return activation, weight_grad.reshape(local_blocks, width), bias_grad.reshape(-1)


def body(tokens, w_blocks, hidden_bias, pattern, grad_act):
    rows = lax.axis_size("row")
    piece = w_blocks.shape[1] // BLK
    fits = lax.axis_size("col") == 2 and rows % 4 == 0 and rows > 4
    fits = fits and piece % 8 == 0 and w_blocks.shape[0] % 4 == 0
    run = kernel_body if fits else plain_body
    return run(tokens, w_blocks, hidden_bias, pattern, grad_act)


def solution(mesh):
    return jax.shard_map(
        body,
        mesh=mesh,
        in_specs=(P("row", "col"), P("col", "row"), P("col"), P(), P("row", "col")),
        out_specs=(P("row", "col"), P("col", "row"), P("col")),
        check_vma=False,
    )
```

```python
import functools
import math

import jax
import jax.numpy as jnp
from jax import lax
from jax.experimental import pallas as pl
from jax.experimental.pallas import tpu as pltpu
from jax.sharding import PartitionSpec as P

BLK = 128
LEVELS = 3
GLOB = 2
KSLOT = 5
MESH = pl.DeviceIdType.MESH
VMEM_LIMIT = 60 * 1024 * 1024


def from_behind(block, axis, distance):
    devices = range(lax.axis_size(axis))
    route = [((i - distance) % len(devices), i) for i in devices]
    return lax.ppermute(block, axis, route)


def broadcast(value, axis, source):
    kept = jnp.where(lax.axis_index(axis) == source, value, 0).astype(value.dtype)
    return lax.psum(kept, axis)


def plain_body(tokens, w_blocks, hidden_bias, pattern, grad_act):
    tok_rows = tokens.shape[0]
    local_blocks = w_blocks.shape[0]
    col_count = lax.axis_size("col")
    col_index = lax.axis_index("col")
    panel_blocks = tokens.shape[1] // BLK
    inv_scale = 1.0 / math.sqrt(tok_rows * lax.axis_size("row"))
    gathered_weights = lax.all_gather(w_blocks, "row", axis=1, tiled=True)
    weights = gathered_weights.reshape(local_blocks, KSLOT, BLK, BLK)
    my_pattern = lax.dynamic_slice_in_dim(pattern, col_index * local_blocks, local_blocks, 0)
    own_panel = tokens.reshape(tok_rows, panel_blocks, BLK)
    pieces = [jnp.take(own_panel, my_pattern[:, 0] - col_index * panel_blocks, axis=1)]
    for level_index in range(LEVELS):
        offset = 2**level_index % col_count
        if offset == 0:
            source = own_panel
        else:
            moved = from_behind(tokens, "col", -offset)
            source = moved.reshape(tok_rows, panel_blocks, BLK)
        home_panel = (col_index + offset) % col_count
        pieces.append(
            jnp.take(source, my_pattern[:, level_index + 1] - home_panel * panel_blocks, axis=1)
        )
    shared = broadcast(tokens[:, : GLOB * BLK], "col", 0).reshape(tok_rows, GLOB, BLK)
    pieces.append(jnp.take(shared, my_pattern[:, LEVELS + 1], axis=1))
    picked = jnp.stack(pieces, axis=2)
    pre_act = jnp.einsum("thkc,hkcd->thd", picked, weights, preferred_element_type=jnp.float32)
    pre_act = pre_act + hidden_bias.astype(jnp.float32).reshape(local_blocks, BLK)
    act_value, pull_back = jax.vjp(jax.nn.gelu, pre_act)
    activation = act_value.reshape(tok_rows, local_blocks * BLK).astype(jnp.bfloat16)
    grad_pre = pull_back(grad_act.astype(jnp.float32).reshape(tok_rows, local_blocks, BLK))[0]
    grad_rounded = grad_pre.astype(jnp.bfloat16)
    weight_terms = (
        jnp.einsum("thkc,thd->hkcd", picked, grad_rounded, preferred_element_type=jnp.float32)
        * inv_scale
    )
    weight_terms = weight_terms.reshape(local_blocks, KSLOT * BLK * BLK)
    weight_grad = lax.psum_scatter(weight_terms, "row", scatter_dimension=1, tiled=True)
    bias_terms = jnp.sum(grad_pre, axis=0).reshape(local_blocks * BLK) * inv_scale
    bias_grad = lax.psum(bias_terms, "row")
    return (activation, weight_grad, bias_grad)


def place(quads):
    row = lax.axis_index("row")
    return row, row // 4, (row // 2) % 2, row % 2, lax.axis_index("col")


def greet(row, quad, bit_y, bit_x, col, quads, extra=()):
    barrier = pltpu.get_barrier_semaphore()
    peers = [(quad * 4 + bit_y * 2 + 1 - bit_x, col), (quad * 4 + (1 - bit_y) * 2 + bit_x, col)]
    peers += [((quad + d) % quads * 4 + bit_y * 2 + bit_x, col) for d in range(1, quads)]
    peers += list(extra)
    for peer in peers:
        pl.semaphore_signal(barrier, inc=1, device_id=peer, device_id_type=MESH)
    pl.semaphore_wait(barrier, len(peers))


def gather_kernel(quads, w_ref, tok_ref, all_ref, peer_ref,
                  own_sem, tok_s, tok_r, z_s, z_r, y_s, y_r, x_s, x_r):
    row, quad, bit_y, bit_x, col = place(quads)
    half = w_ref.shape[0] // 2
    x_peer = (quad * 4 + bit_y * 2 + 1 - bit_x, col)
    y_peer = (quad * 4 + (1 - bit_y) * 2 + bit_x, col)
    greet(row, quad, bit_y, bit_x, col, quads, [(row, 1 - col)])

    def send(src, dst, s, r, peer):
        copy = pltpu.make_async_remote_copy(
            src_ref=src, dst_ref=dst, send_sem=s, recv_sem=r, device_id=peer, device_id_type=MESH
        )
        copy.start()
        return copy

    copies = []
    own = pltpu.make_async_copy(w_ref, all_ref.at[row], own_sem)
    own.start()
    z_copies = []
    for d in range(1, quads):
        target = ((quad + d) % quads * 4 + bit_y * 2 + bit_x, col)
        z_copies.append(send(w_ref, all_ref.at[row], z_s.at[d - 1], z_r.at[d - 1], target))
    cut = [pl.ds(0, half), pl.ds(half, half)]
    first_y, first_x = [], []
    for d in range(quads):
        src_row = (quad - d + quads) % quads * 4 + bit_y * 2 + bit_x
        if d > 0:
            z_copies[d - 1].wait_recv()
        src = [w_ref.at[c] if d == 0 else all_ref.at[src_row, c] for c in cut]
        dst = [all_ref.at[src_row, c] for c in cut]
        first_y.append(send(src[0], dst[0], y_s.at[d], y_r.at[d], y_peer))
        first_x.append(send(src[1], dst[1], x_s.at[d], x_r.at[d], x_peer))
        copies.append(send(src[0], dst[0], x_s.at[quads + d], x_r.at[quads + d], x_peer))
        copies.append(send(src[1], dst[1], y_s.at[quads + d], y_r.at[quads + d], y_peer))
        if d == 0:
            tok_copy = send(tok_ref, peer_ref, tok_s, tok_r, (row, 1 - col))
    for d in range(quads):
        from_quad = (quad - d + quads) % quads * 4
        y_row = from_quad + (1 - bit_y) * 2 + bit_x
        x_row = from_quad + bit_y * 2 + 1 - bit_x
        first_y[d].wait_recv()
        piece = all_ref.at[y_row, cut[0]]
        copies.append(send(piece, piece, x_s.at[2 * quads + d], x_r.at[2 * quads + d], x_peer))
        first_x[d].wait_recv()
        piece = all_ref.at[x_row, cut[1]]
        copies.append(send(piece, piece, y_s.at[2 * quads + d], y_r.at[2 * quads + d], y_peer))
    for copy in copies:
        copy.wait()
    for copy in z_copies + first_y + first_x:
        copy.wait_send()
    tok_copy.wait()
    own.wait()


def gather(w_flat, tokens, quads):
    any_spec = pl.BlockSpec(memory_space=pl.ANY)
    dma = pltpu.SemaphoreType.DMA
    return pl.pallas_call(
        functools.partial(gather_kernel, quads),
        out_shape=(
            jax.ShapeDtypeStruct((quads * 4,) + w_flat.shape, w_flat.dtype),
            jax.ShapeDtypeStruct(tokens.shape, tokens.dtype),
        ),
        in_specs=[pl.BlockSpec(memory_space=pltpu.VMEM), any_spec],
        out_specs=(any_spec, any_spec),
        scratch_shapes=[dma, dma, dma, dma((quads - 1,)), dma((quads - 1,)),
                        dma((3 * quads,)), dma((3 * quads,)), dma((3 * quads,)), dma((3 * quads,))],
        compiler_params=pltpu.CompilerParams(collective_id=0, has_side_effects=True,
                                             vmem_limit_bytes=VMEM_LIMIT),
    )(w_flat, tokens)


def fused_kernel(quads, chunks, blk_rows, strip, scale,
                 pat_ref, own_ref, peer_ref, w_ref, bias_ref, grad_ref,
                 act_ref, out_ref, bout_ref,
                 table, p_ref, b_ref, first, second, second_out, third, third_out,
                 bx, by, by_out, bz, bz_out,
                 f_s, f_r, s_s, s_r, t_s, t_r, b_s, b_r):
    step = pl.program_id(0)
    steps = pl.num_programs(0)
    rows = quads * 4
    row, quad, bit_y, bit_x, col = place(quads)
    n = first.shape[3]
    half = p_ref.shape[1] // 2
    per = p_ref.shape[1] // chunks // (2 * blk_rows)
    peers = [(quad * 4 + bit_y * 2 + 1 - bit_x, col), (quad * 4 + (1 - bit_y) * 2 + bit_x, col)]

    @pl.when(step == 0)
    def _():
        greet(row, quad, bit_y, bit_x, col, quads)

        panel = own_ref.shape[1] // BLK
        for i in range(panel):
            table[col * panel + i] = own_ref[:, i * BLK:(i + 1) * BLK]
            table[(1 - col) * panel + i] = peer_ref[:, i * BLK:(i + 1) * BLK]

    pair = pair_of(step, per, chunks)
    weights = [w_ref[r].astype(jnp.float32) for r in range(rows)]
    results = []
    for j in range(2):
        piece = pl.ds(j * BLK, BLK)
        w = jnp.concatenate([v[j * blk_rows:(j + 1) * blk_rows] for v in weights], axis=0)
        w = w.astype(jnp.bfloat16)
        base = (2 * pair + j) * KSLOT
        picks = [table[pat_ref[base + k]] for k in range(KSLOT)]
        sel = jnp.concatenate(picks, axis=1)
        v = jnp.dot(sel, w, preferred_element_type=jnp.float32)
        v = v + bias_ref[:, piece].astype(jnp.float32)
        c = math.sqrt(2.0 / math.pi)
        sq = v * v
        t = jnp.tanh(v * (c + (c * 0.044715) * sq))
        lift = 0.5 + 0.5 * t
        act_ref[:, piece] = (v * lift).astype(jnp.bfloat16)
        slope = lift + (0.5 * v) * (1.0 - t * t) * (c + (3.0 * 0.044715 * c) * sq)
        grad = grad_ref[:, piece].astype(jnp.float32) * slope
        b_ref[pl.ds(2 * pair + j, 1), :] = jnp.sum(grad, axis=0, keepdims=True) * scale
        out = lax.dot_general(sel, grad.astype(jnp.bfloat16), (((0,), (0,)), ((), ())),
                              preferred_element_type=jnp.float32)
        results.append(out * scale)
    at = pl.multiple_of(pair * (2 * blk_rows), 2 * blk_rows)
    for r in range(rows):
        cut = slice(r * blk_rows, (r + 1) * blk_rows)
        p_ref[r, pl.ds(at, 2 * blk_rows), :] = jnp.concatenate(
            [o[cut] for o in results], axis=0).astype(p_ref.dtype)

    def link(src, dst, s, r, peer):
        return pltpu.make_async_remote_copy(
            src_ref=src, dst_ref=dst, send_sem=s, recv_sem=r, device_id=peer, device_id_type=MESH
        )

    def piece_row(d, colour, near, far):
        flip_x, flip_y = (near, far) if colour == 0 else (far, near)
        x = (1 - bit_x) if flip_x else bit_x
        y = (1 - bit_y) if flip_y else bit_y
        return (quad + d) % quads * 4 + y * 2 + x

    order = list(range(1, quads)) + [0]
    start = lambda c: (c % 2) * half + (c // 2) * n

    def first_copy(c, far, d):
        return link(p_ref.at[piece_row(d, c % 2, 1, far), pl.ds(start(c), n)],
                    first.at[c, far, d], f_s.at[c, far, d], f_r.at[c, far, d], peers[c % 2])

    def second_copy(c, d):
        return link(second_out.at[c, d], second.at[c, d], s_s.at[c, d], s_r.at[c, d],
                    peers[1 - c % 2])

    def third_copy(c, d):
        target = ((quad + d) % quads * 4 + bit_y * 2 + bit_x, col)
        return link(third_out.at[c, d - 1], third.at[c, d - 1],
                    t_s.at[c, d - 1], t_r.at[c, d - 1], target)

    def do_first(c):
        for far in (1, 0):
            for d in order:
                first_copy(c, far, d).start()

    def do_second(c):
        for d in order:
            first_copy(c, 1, d).wait_recv()
            mine = piece_row(d, c % 2, 0, 1)

            @pl.loop(0, n // strip)
            def _(i, d=d, mine=mine):
                s = pl.multiple_of(i * strip, strip)
                here = p_ref[mine, pl.ds(start(c) + s, strip), :].astype(jnp.float32)
                come = first[c, 1, d, pl.ds(s, strip), :].astype(jnp.float32)
                second_out[c, d, pl.ds(s, strip), :] = (here + come).astype(jnp.bfloat16)

            second_copy(c, d).start()

    def do_third(c):
        for d in order:
            first_copy(c, 0, d).wait_recv()
            second_copy(c, d).wait_recv()
            mine = piece_row(d, c % 2, 0, 0)

            @pl.loop(0, n // strip)
            def _(i, d=d, mine=mine):
                s = pl.multiple_of(i * strip, strip)
                total = p_ref[mine, pl.ds(start(c) + s, strip), :].astype(jnp.float32)
                total += first[c, 0, d, pl.ds(s, strip), :].astype(jnp.float32)
                total += second[c, d, pl.ds(s, strip), :].astype(jnp.float32)
                if d == 0:
                    out_ref[pl.ds(start(c) + s, strip), :] = total
                else:
                    third_out[c, d - 1, pl.ds(s, strip), :] = total.astype(jnp.bfloat16)

            if d > 0:
                third_copy(c, d).start()

    for c in range(chunks):
        @pl.when(step == (c + 1) * per - 1)
        def _(c=c):
            do_first(c)
            if c >= 2 and c < chunks - 1:
                do_second(c - 2)

    @pl.when(step == steps - 1)
    def _():
        to_x = link(b_ref, bx, b_s.at[0], b_r.at[0], peers[0])
        to_x.start()
        do_second(chunks - 3)
        do_second(chunks - 2)
        to_x.wait()
        by_out[...] = b_ref[...] + bx[...]
        to_y = link(by_out, by, b_s.at[1], b_r.at[1], peers[1])
        to_y.start()
        do_third(0)
        do_second(chunks - 1)
        to_y.wait()
        bz_out[...] = by_out[...] + by[...]
        to_z = []
        for d in range(1, quads):
            target = ((quad + d) % quads * 4 + bit_y * 2 + bit_x, col)
            to_z.append(link(bz_out, bz.at[d - 1], b_s.at[d + 1], b_r.at[d + 1], target))
            to_z[-1].start()
        for c in range(1, chunks):
            do_third(c)
        for copy in to_z:
            copy.wait()
        total = bz_out[...]
        for d in range(quads - 1):
            total += bz[d]
        bout_ref[...] = total
        for c in range(chunks):
            for d in range(1, quads):
                third_copy(c, d).wait()

            @pl.loop(0, n // strip)
            def _(i, c=c):
                s = pl.multiple_of(i * strip, strip)
                total = out_ref[pl.ds(start(c) + s, strip), :]
                for d in range(quads - 1):
                    total += third[c, d, pl.ds(s, strip), :].astype(jnp.float32)
                out_ref[pl.ds(start(c) + s, strip), :] = total
        for c in range(chunks):
            for d in order:
                first_copy(c, 0, d).wait_send()
                first_copy(c, 1, d).wait_send()
                second_copy(c, d).wait_send()


def pair_of(step, per, chunks):
    chunk = step // per
    return (chunk % 2) * (per * chunks // 2) + (chunk // 2) * per + step % per


def fused(pat, own, peer, weights, bias, grad_act, quads, scale):
    tok, hidden = grad_act.shape
    blocks = hidden // BLK
    steps = blocks // 2
    chunks = 4
    per = steps // chunks
    total_rows = weights.shape[1]
    blk_rows = total_rows // blocks
    n = total_rows // chunks
    strip = next(c for c in (160, 128, 96, 80, 64, 48, 32, 16) if n % c == 0)
    rows = quads * 4
    whole = lambda a: pl.BlockSpec(a.shape, lambda i, p: (0, 0))
    wide = lambda m: pl.BlockSpec((m, 2 * BLK), lambda i, p: (0, pair_of(i, per, chunks)))
    fixed = lambda *s: pl.BlockSpec(s, lambda i, p: (0, 0))
    cube = pl.BlockSpec((rows, 2 * blk_rows, BLK), lambda i, p: (0, pair_of(i, per, chunks), 0))
    dma = pltpu.SemaphoreType.DMA
    bf = lambda *s: pltpu.VMEM(s, jnp.bfloat16)
    f32 = lambda *s: pltpu.VMEM(s, jnp.float32)
    b = (blocks, BLK)
    return pl.pallas_call(
        functools.partial(fused_kernel, quads, chunks, blk_rows, strip, scale),
        out_shape=(
            jax.ShapeDtypeStruct((tok, hidden), jnp.bfloat16),
            jax.ShapeDtypeStruct((total_rows, BLK), jnp.float32),
            jax.ShapeDtypeStruct(b, jnp.float32),
        ),
        grid_spec=pltpu.PrefetchScalarGridSpec(
            num_scalar_prefetch=1, grid=(steps,),
            in_specs=[whole(own), whole(peer), cube, wide(1), wide(tok)],
            out_specs=[wide(tok), fixed(total_rows, BLK), fixed(*b)],
            scratch_shapes=[
                bf(2 * own.shape[1] // BLK, tok, BLK), bf(rows, total_rows, BLK), f32(*b),
                bf(chunks, 2, quads, n, BLK), bf(chunks, quads, n, BLK), bf(chunks, quads, n, BLK),
                bf(chunks, quads - 1, n, BLK), bf(chunks, quads - 1, n, BLK),
                f32(*b), f32(*b), f32(*b), f32(quads - 1, *b), f32(*b),
                dma((chunks, 2, quads)), dma((chunks, 2, quads)), dma((chunks, quads)),
                dma((chunks, quads)), dma((chunks, quads - 1)), dma((chunks, quads - 1)),
                dma((quads + 1,)), dma((quads + 1,)),
            ],
        ),
        compiler_params=pltpu.CompilerParams(collective_id=1, has_side_effects=True,
                                             vmem_limit_bytes=VMEM_LIMIT),
    )(pat, own, peer, weights, bias, grad_act)


def kernel_body(tokens, w_blocks, hidden_bias, pattern, grad_act):
    tok_rows = tokens.shape[0]
    local_blocks, width = w_blocks.shape
    rows = lax.axis_size("row")
    quads = rows // 4
    col = lax.axis_index("col")
    scale = 1.0 / math.sqrt(tok_rows * rows)
    pat = lax.dynamic_slice_in_dim(pattern, col * local_blocks, local_blocks, 0).reshape(-1)
    flat = w_blocks.reshape(local_blocks * width // BLK, BLK)
    weights, peer = gather(flat, tokens, quads)
    activation, weight_grad, bias_grad = fused(
        pat, tokens, peer, weights, hidden_bias.reshape(1, -1), grad_act, quads, scale)
    return activation, weight_grad.reshape(local_blocks, width), bias_grad.reshape(-1)


def body(tokens, w_blocks, hidden_bias, pattern, grad_act):
    rows = lax.axis_size("row")
    piece = w_blocks.shape[1] // BLK
    fits = lax.axis_size("col") == 2 and rows % 4 == 0 and rows > 4
    fits = fits and piece % 8 == 0 and w_blocks.shape[0] % 8 == 0
    run = kernel_body if fits else plain_body
    return run(tokens, w_blocks, hidden_bias, pattern, grad_act)


def solution(mesh):
    return jax.shard_map(
        body,
        mesh=mesh,
        in_specs=(P("row", "col"), P("col", "row"), P("col"), P(), P("row", "col")),
        out_specs=(P("row", "col"), P("col", "row"), P("col")),
        check_vma=False,
    )
```

```python
import functools
import math

import jax
import jax.numpy as jnp
from jax import lax
from jax.experimental import pallas as pl
from jax.experimental.pallas import tpu as pltpu
from jax.sharding import PartitionSpec as P

BLK = 128
LEVELS = 3
GLOB = 2
KSLOT = 5
MESH = pl.DeviceIdType.MESH
VMEM_LIMIT = 60 * 1024 * 1024


def from_behind(block, axis, distance):
    devices = range(lax.axis_size(axis))
    route = [((i - distance) % len(devices), i) for i in devices]
    return lax.ppermute(block, axis, route)


def broadcast(value, axis, source):
    kept = jnp.where(lax.axis_index(axis) == source, value, 0).astype(value.dtype)
    return lax.psum(kept, axis)


def plain_body(tokens, w_blocks, hidden_bias, pattern, grad_act):
    tok_rows = tokens.shape[0]
    local_blocks = w_blocks.shape[0]
    col_count = lax.axis_size("col")
    col_index = lax.axis_index("col")
    panel_blocks = tokens.shape[1] // BLK
    inv_scale = 1.0 / math.sqrt(tok_rows * lax.axis_size("row"))
    gathered_weights = lax.all_gather(w_blocks, "row", axis=1, tiled=True)
    weights = gathered_weights.reshape(local_blocks, KSLOT, BLK, BLK)
    my_pattern = lax.dynamic_slice_in_dim(pattern, col_index * local_blocks, local_blocks, 0)
    own_panel = tokens.reshape(tok_rows, panel_blocks, BLK)
    pieces = [jnp.take(own_panel, my_pattern[:, 0] - col_index * panel_blocks, axis=1)]
    for level_index in range(LEVELS):
        offset = 2**level_index % col_count
        if offset == 0:
            source = own_panel
        else:
            moved = from_behind(tokens, "col", -offset)
            source = moved.reshape(tok_rows, panel_blocks, BLK)
        home_panel = (col_index + offset) % col_count
        pieces.append(
            jnp.take(source, my_pattern[:, level_index + 1] - home_panel * panel_blocks, axis=1)
        )
    shared = broadcast(tokens[:, : GLOB * BLK], "col", 0).reshape(tok_rows, GLOB, BLK)
    pieces.append(jnp.take(shared, my_pattern[:, LEVELS + 1], axis=1))
    picked = jnp.stack(pieces, axis=2)
    pre_act = jnp.einsum("thkc,hkcd->thd", picked, weights, preferred_element_type=jnp.float32)
    pre_act = pre_act + hidden_bias.astype(jnp.float32).reshape(local_blocks, BLK)
    act_value, pull_back = jax.vjp(jax.nn.gelu, pre_act)
    activation = act_value.reshape(tok_rows, local_blocks * BLK).astype(jnp.bfloat16)
    grad_pre = pull_back(grad_act.astype(jnp.float32).reshape(tok_rows, local_blocks, BLK))[0]
    grad_rounded = grad_pre.astype(jnp.bfloat16)
    weight_terms = (
        jnp.einsum("thkc,thd->hkcd", picked, grad_rounded, preferred_element_type=jnp.float32)
        * inv_scale
    )
    weight_terms = weight_terms.reshape(local_blocks, KSLOT * BLK * BLK)
    weight_grad = lax.psum_scatter(weight_terms, "row", scatter_dimension=1, tiled=True)
    bias_terms = jnp.sum(grad_pre, axis=0).reshape(local_blocks * BLK) * inv_scale
    bias_grad = lax.psum(bias_terms, "row")
    return (activation, weight_grad, bias_grad)


def place(quads):
    row = lax.axis_index("row")
    return row, row // 4, (row // 2) % 2, row % 2, lax.axis_index("col")


def greet(row, quad, bit_y, bit_x, col, quads, extra=()):
    barrier = pltpu.get_barrier_semaphore()
    peers = [(quad * 4 + bit_y * 2 + 1 - bit_x, col), (quad * 4 + (1 - bit_y) * 2 + bit_x, col)]
    peers += [((quad + d) % quads * 4 + bit_y * 2 + bit_x, col) for d in range(1, quads)]
    peers += list(extra)
    for peer in peers:
        pl.semaphore_signal(barrier, inc=1, device_id=peer, device_id_type=MESH)
    pl.semaphore_wait(barrier, len(peers))


def gather_kernel(quads, w_ref, tok_ref, all_ref, peer_ref,
                  own_sem, tok_s, tok_r, z_s, z_r, y_s, y_r, x_s, x_r):
    row, quad, bit_y, bit_x, col = place(quads)
    half = w_ref.shape[0] // 2
    x_peer = (quad * 4 + bit_y * 2 + 1 - bit_x, col)
    y_peer = (quad * 4 + (1 - bit_y) * 2 + bit_x, col)
    greet(row, quad, bit_y, bit_x, col, quads, [(row, 1 - col)])

    def send(src, dst, s, r, peer):
        copy = pltpu.make_async_remote_copy(
            src_ref=src, dst_ref=dst, send_sem=s, recv_sem=r, device_id=peer, device_id_type=MESH
        )
        copy.start()
        return copy

    copies = []
    own = pltpu.make_async_copy(w_ref, all_ref.at[row], own_sem)
    own.start()
    z_copies = []
    for d in range(1, quads):
        target = ((quad + d) % quads * 4 + bit_y * 2 + bit_x, col)
        z_copies.append(send(w_ref, all_ref.at[row], z_s.at[d - 1], z_r.at[d - 1], target))
    cut = [pl.ds(0, half), pl.ds(half, half)]
    first_y, first_x = [], []
    for d in range(quads):
        src_row = (quad - d + quads) % quads * 4 + bit_y * 2 + bit_x
        if d > 0:
            z_copies[d - 1].wait_recv()
        src = [w_ref.at[c] if d == 0 else all_ref.at[src_row, c] for c in cut]
        dst = [all_ref.at[src_row, c] for c in cut]
        first_y.append(send(src[0], dst[0], y_s.at[d], y_r.at[d], y_peer))
        first_x.append(send(src[1], dst[1], x_s.at[d], x_r.at[d], x_peer))
        copies.append(send(src[0], dst[0], x_s.at[quads + d], x_r.at[quads + d], x_peer))
        copies.append(send(src[1], dst[1], y_s.at[quads + d], y_r.at[quads + d], y_peer))
        if d == 0:
            tok_copy = send(tok_ref, peer_ref, tok_s, tok_r, (row, 1 - col))
    for d in range(quads):
        from_quad = (quad - d + quads) % quads * 4
        y_row = from_quad + (1 - bit_y) * 2 + bit_x
        x_row = from_quad + bit_y * 2 + 1 - bit_x
        first_y[d].wait_recv()
        piece = all_ref.at[y_row, cut[0]]
        copies.append(send(piece, piece, x_s.at[2 * quads + d], x_r.at[2 * quads + d], x_peer))
        first_x[d].wait_recv()
        piece = all_ref.at[x_row, cut[1]]
        copies.append(send(piece, piece, y_s.at[2 * quads + d], y_r.at[2 * quads + d], y_peer))
    for copy in copies:
        copy.wait()
    for copy in z_copies + first_y + first_x:
        copy.wait_send()
    tok_copy.wait()
    own.wait()


def gather(w_flat, tokens, quads):
    any_spec = pl.BlockSpec(memory_space=pl.ANY)
    dma = pltpu.SemaphoreType.DMA
    return pl.pallas_call(
        functools.partial(gather_kernel, quads),
        out_shape=(
            jax.ShapeDtypeStruct((quads * 4,) + w_flat.shape, w_flat.dtype),
            jax.ShapeDtypeStruct(tokens.shape, tokens.dtype),
        ),
        in_specs=[pl.BlockSpec(memory_space=pltpu.VMEM), any_spec],
        out_specs=(any_spec, any_spec),
        scratch_shapes=[dma, dma, dma, dma((quads - 1,)), dma((quads - 1,)),
                        dma((3 * quads,)), dma((3 * quads,)), dma((3 * quads,)), dma((3 * quads,))],
        compiler_params=pltpu.CompilerParams(collective_id=0, has_side_effects=True,
                                             vmem_limit_bytes=VMEM_LIMIT),
    )(w_flat, tokens)


def fused_kernel(quads, chunks, blk_rows, strip, scale,
                 pat_ref, own_ref, peer_ref, w_ref, bias_ref, grad_ref,
                 act_ref, out_ref, bout_ref,
                 table, p_ref, b_ref, first, second, second_out, third, third_out,
                 bx, by, by_out, bz, bz_out,
                 f_s, f_r, s_s, s_r, t_s, t_r, b_s, b_r):
    step = pl.program_id(0)
    steps = pl.num_programs(0)
    rows = quads * 4
    row, quad, bit_y, bit_x, col = place(quads)
    n = first.shape[3]
    half = p_ref.shape[1] // 2
    per = p_ref.shape[1] // chunks // (2 * blk_rows)
    peers = [(quad * 4 + bit_y * 2 + 1 - bit_x, col), (quad * 4 + (1 - bit_y) * 2 + bit_x, col)]

    @pl.when(step == 0)
    def _():
        greet(row, quad, bit_y, bit_x, col, quads)

        panel = own_ref.shape[1] // BLK
        for i in range(panel):
            table[col * panel + i] = own_ref[:, i * BLK:(i + 1) * BLK]
            table[(1 - col) * panel + i] = peer_ref[:, i * BLK:(i + 1) * BLK]

    pair = pair_of(step, per, chunks)
    weights = [w_ref[r].astype(jnp.float32) for r in range(rows)]
    results = []
    for j in range(2):
        piece = pl.ds(j * BLK, BLK)
        w = jnp.concatenate([v[j * blk_rows:(j + 1) * blk_rows] for v in weights], axis=0)
        w = w.astype(jnp.bfloat16)
        base = (2 * pair + j) * KSLOT
        picks = [table[pat_ref[base + k]] for k in range(KSLOT)]
        sel = jnp.concatenate(picks, axis=1)
        v = jnp.dot(sel, w, preferred_element_type=jnp.float32)
        v = v + bias_ref[:, piece].astype(jnp.float32)
        c = math.sqrt(2.0 / math.pi)
        sq = v * v
        t = jnp.tanh(v * (c + (c * 0.044715) * sq))
        lift = 0.5 + 0.5 * t
        act_ref[:, piece] = (v * lift).astype(jnp.bfloat16)
        slope = lift + (0.5 * v) * (1.0 - t * t) * (c + (3.0 * 0.044715 * c) * sq)
        grad = grad_ref[:, piece].astype(jnp.float32) * slope
        b_ref[pl.ds(2 * pair + j, 1), :] = jnp.sum(grad, axis=0, keepdims=True) * scale
        out = lax.dot_general(sel, grad.astype(jnp.bfloat16), (((0,), (0,)), ((), ())),
                              preferred_element_type=jnp.float32)
        results.append(out * scale)
    at = pl.multiple_of(pair * (2 * blk_rows), 2 * blk_rows)
    for r in range(rows):
        cut = slice(r * blk_rows, (r + 1) * blk_rows)
        p_ref[r, pl.ds(at, 2 * blk_rows), :] = jnp.concatenate(
            [o[cut] for o in results], axis=0).astype(p_ref.dtype)

    def link(src, dst, s, r, peer):
        return pltpu.make_async_remote_copy(
            src_ref=src, dst_ref=dst, send_sem=s, recv_sem=r, device_id=peer, device_id_type=MESH
        )

    def piece_row(d, colour, near, far):
        flip_x, flip_y = (near, far) if colour == 0 else (far, near)
        x = (1 - bit_x) if flip_x else bit_x
        y = (1 - bit_y) if flip_y else bit_y
        return (quad + d) % quads * 4 + y * 2 + x

    order = list(range(1, quads)) + [0]
    start = lambda c: (c % 2) * half + (c // 2) * n

    def first_copy(c, far, d):
        return link(p_ref.at[piece_row(d, c % 2, 1, far), pl.ds(start(c), n)],
                    first.at[c, far, d], f_s.at[c, far, d], f_r.at[c, far, d], peers[c % 2])

    def second_copy(c, d):
        return link(second_out.at[c, d], second.at[c, d], s_s.at[c, d], s_r.at[c, d],
                    peers[1 - c % 2])

    def third_copy(c, d):
        target = ((quad + d) % quads * 4 + bit_y * 2 + bit_x, col)
        return link(third_out.at[c, d - 1], third.at[c, d - 1],
                    t_s.at[c, d - 1], t_r.at[c, d - 1], target)

    def do_first(c):
        for far in (1, 0):
            for d in order:
                first_copy(c, far, d).start()

    def do_second(c):
        for d in order:
            first_copy(c, 1, d).wait_recv()
            mine = piece_row(d, c % 2, 0, 1)

            @pl.loop(0, n // strip)
            def _(i, d=d, mine=mine):
                s = pl.multiple_of(i * strip, strip)
                here = p_ref[mine, pl.ds(start(c) + s, strip), :].astype(jnp.float32)
                come = first[c, 1, d, pl.ds(s, strip), :].astype(jnp.float32)
                second_out[c, d, pl.ds(s, strip), :] = (here + come).astype(jnp.bfloat16)

            second_copy(c, d).start()

    def do_third(c):
        for d in order:
            first_copy(c, 0, d).wait_recv()
            second_copy(c, d).wait_recv()
            mine = piece_row(d, c % 2, 0, 0)

            @pl.loop(0, n // strip)
            def _(i, d=d, mine=mine):
                s = pl.multiple_of(i * strip, strip)
                total = p_ref[mine, pl.ds(start(c) + s, strip), :].astype(jnp.float32)
                total += first[c, 0, d, pl.ds(s, strip), :].astype(jnp.float32)
                total += second[c, d, pl.ds(s, strip), :].astype(jnp.float32)
                if d == 0:
                    out_ref[pl.ds(start(c) + s, strip), :] = total
                else:
                    third_out[c, d - 1, pl.ds(s, strip), :] = total.astype(jnp.bfloat16)

            if d > 0:
                third_copy(c, d).start()

    for c in range(chunks):
        @pl.when(step == (c + 1) * per - 1)
        def _(c=c):
            do_first(c)
            if c >= 2:
                do_second(c - 2)
            if c >= 4:
                do_third(c - 4)

    @pl.when(step == steps - 1)
    def _():
        to_x = link(b_ref, bx, b_s.at[0], b_r.at[0], peers[0])
        to_x.start()
        do_second(chunks - 2)
        do_third(chunks - 4)
        to_x.wait()
        by_out[...] = b_ref[...] + bx[...]
        to_y = link(by_out, by, b_s.at[1], b_r.at[1], peers[1])
        to_y.start()
        do_second(chunks - 1)
        do_third(chunks - 3)
        to_y.wait()
        bz_out[...] = by_out[...] + by[...]
        to_z = []
        for d in range(1, quads):
            target = ((quad + d) % quads * 4 + bit_y * 2 + bit_x, col)
            to_z.append(link(bz_out, bz.at[d - 1], b_s.at[d + 1], b_r.at[d + 1], target))
            to_z[-1].start()
        do_third(chunks - 2)
        do_third(chunks - 1)
        for copy in to_z:
            copy.wait()
        total = bz_out[...]
        for d in range(quads - 1):
            total += bz[d]
        bout_ref[...] = total
        for c in range(chunks):
            for d in range(1, quads):
                third_copy(c, d).wait()

            @pl.loop(0, n // strip)
            def _(i, c=c):
                s = pl.multiple_of(i * strip, strip)
                total = out_ref[pl.ds(start(c) + s, strip), :]
                for d in range(quads - 1):
                    total += third[c, d, pl.ds(s, strip), :].astype(jnp.float32)
                out_ref[pl.ds(start(c) + s, strip), :] = total
        for c in range(chunks):
            for d in order:
                first_copy(c, 0, d).wait_send()
                first_copy(c, 1, d).wait_send()
                second_copy(c, d).wait_send()


def pair_of(step, per, chunks):
    chunk = step // per
    return (chunk % 2) * (per * chunks // 2) + (chunk // 2) * per + step % per


def fused(pat, own, peer, weights, bias, grad_act, quads, scale):
    tok, hidden = grad_act.shape
    blocks = hidden // BLK
    steps = blocks // 2
    total_rows = weights.shape[1]
    chunks = 8 if steps % 8 == 0 and total_rows % 128 == 0 else 4
    per = steps // chunks
    blk_rows = total_rows // blocks
    n = total_rows // chunks
    strip = next(c for c in (240, 160, 128, 96, 80, 64, 48, 32, 16) if n % c == 0)
    rows = quads * 4
    whole = lambda a: pl.BlockSpec(a.shape, lambda i, p: (0, 0))
    wide = lambda m: pl.BlockSpec((m, 2 * BLK), lambda i, p: (0, pair_of(i, per, chunks)))
    fixed = lambda *s: pl.BlockSpec(s, lambda i, p: (0, 0))
    cube = pl.BlockSpec((rows, 2 * blk_rows, BLK), lambda i, p: (0, pair_of(i, per, chunks), 0))
    dma = pltpu.SemaphoreType.DMA
    bf = lambda *s: pltpu.VMEM(s, jnp.bfloat16)
    f32 = lambda *s: pltpu.VMEM(s, jnp.float32)
    b = (blocks, BLK)
    return pl.pallas_call(
        functools.partial(fused_kernel, quads, chunks, blk_rows, strip, scale),
        out_shape=(
            jax.ShapeDtypeStruct((tok, hidden), jnp.bfloat16),
            jax.ShapeDtypeStruct((total_rows, BLK), jnp.float32),
            jax.ShapeDtypeStruct(b, jnp.float32),
        ),
        grid_spec=pltpu.PrefetchScalarGridSpec(
            num_scalar_prefetch=1, grid=(steps,),
            in_specs=[whole(own), whole(peer), cube, wide(1), wide(tok)],
            out_specs=[wide(tok), fixed(total_rows, BLK), fixed(*b)],
            scratch_shapes=[
                bf(2 * own.shape[1] // BLK, tok, BLK), bf(rows, total_rows, BLK), f32(*b),
                bf(chunks, 2, quads, n, BLK), bf(chunks, quads, n, BLK), bf(chunks, quads, n, BLK),
                bf(chunks, quads - 1, n, BLK), bf(chunks, quads - 1, n, BLK),
                f32(*b), f32(*b), f32(*b), f32(quads - 1, *b), f32(*b),
                dma((chunks, 2, quads)), dma((chunks, 2, quads)), dma((chunks, quads)),
                dma((chunks, quads)), dma((chunks, quads - 1)), dma((chunks, quads - 1)),
                dma((quads + 1,)), dma((quads + 1,)),
            ],
        ),
        compiler_params=pltpu.CompilerParams(collective_id=1, has_side_effects=True,
                                             vmem_limit_bytes=VMEM_LIMIT),
    )(pat, own, peer, weights, bias, grad_act)


def kernel_body(tokens, w_blocks, hidden_bias, pattern, grad_act):
    tok_rows = tokens.shape[0]
    local_blocks, width = w_blocks.shape
    rows = lax.axis_size("row")
    quads = rows // 4
    col = lax.axis_index("col")
    scale = 1.0 / math.sqrt(tok_rows * rows)
    pat = lax.dynamic_slice_in_dim(pattern, col * local_blocks, local_blocks, 0).reshape(-1)
    flat = w_blocks.reshape(local_blocks * width // BLK, BLK)
    weights, peer = gather(flat, tokens, quads)
    activation, weight_grad, bias_grad = fused(
        pat, tokens, peer, weights, hidden_bias.reshape(1, -1), grad_act, quads, scale)
    return activation, weight_grad.reshape(local_blocks, width), bias_grad.reshape(-1)


def body(tokens, w_blocks, hidden_bias, pattern, grad_act):
    rows = lax.axis_size("row")
    piece = w_blocks.shape[1] // BLK
    fits = lax.axis_size("col") == 2 and rows % 4 == 0 and rows > 4
    fits = fits and piece % 8 == 0 and w_blocks.shape[0] % 8 == 0
    run = kernel_body if fits else plain_body
    return run(tokens, w_blocks, hidden_bias, pattern, grad_act)


def solution(mesh):
    return jax.shard_map(
        body,
        mesh=mesh,
        in_specs=(P("row", "col"), P("col", "row"), P("col"), P(), P("row", "col")),
        out_specs=(P("row", "col"), P("col", "row"), P("col")),
        check_vma=False,
    )
```

```python
import functools
import math

import jax
import jax.numpy as jnp
from jax import lax
from jax.experimental import pallas as pl
from jax.experimental.pallas import tpu as pltpu
from jax.sharding import PartitionSpec as P

BLK = 128
LEVELS = 3
GLOB = 2
KSLOT = 5
MESH = pl.DeviceIdType.MESH
VMEM_LIMIT = 60 * 1024 * 1024


def from_behind(block, axis, distance):
    devices = range(lax.axis_size(axis))
    route = [((i - distance) % len(devices), i) for i in devices]
    return lax.ppermute(block, axis, route)


def broadcast(value, axis, source):
    kept = jnp.where(lax.axis_index(axis) == source, value, 0).astype(value.dtype)
    return lax.psum(kept, axis)


def plain_body(tokens, w_blocks, hidden_bias, pattern, grad_act):
    tok_rows = tokens.shape[0]
    local_blocks = w_blocks.shape[0]
    col_count = lax.axis_size("col")
    col_index = lax.axis_index("col")
    panel_blocks = tokens.shape[1] // BLK
    inv_scale = 1.0 / math.sqrt(tok_rows * lax.axis_size("row"))
    gathered_weights = lax.all_gather(w_blocks, "row", axis=1, tiled=True)
    weights = gathered_weights.reshape(local_blocks, KSLOT, BLK, BLK)
    my_pattern = lax.dynamic_slice_in_dim(pattern, col_index * local_blocks, local_blocks, 0)
    own_panel = tokens.reshape(tok_rows, panel_blocks, BLK)
    pieces = [jnp.take(own_panel, my_pattern[:, 0] - col_index * panel_blocks, axis=1)]
    for level_index in range(LEVELS):
        offset = 2**level_index % col_count
        if offset == 0:
            source = own_panel
        else:
            moved = from_behind(tokens, "col", -offset)
            source = moved.reshape(tok_rows, panel_blocks, BLK)
        home_panel = (col_index + offset) % col_count
        pieces.append(
            jnp.take(source, my_pattern[:, level_index + 1] - home_panel * panel_blocks, axis=1)
        )
    shared = broadcast(tokens[:, : GLOB * BLK], "col", 0).reshape(tok_rows, GLOB, BLK)
    pieces.append(jnp.take(shared, my_pattern[:, LEVELS + 1], axis=1))
    picked = jnp.stack(pieces, axis=2)
    pre_act = jnp.einsum("thkc,hkcd->thd", picked, weights, preferred_element_type=jnp.float32)
    pre_act = pre_act + hidden_bias.astype(jnp.float32).reshape(local_blocks, BLK)
    act_value, pull_back = jax.vjp(jax.nn.gelu, pre_act)
    activation = act_value.reshape(tok_rows, local_blocks * BLK).astype(jnp.bfloat16)
    grad_pre = pull_back(grad_act.astype(jnp.float32).reshape(tok_rows, local_blocks, BLK))[0]
    grad_rounded = grad_pre.astype(jnp.bfloat16)
    weight_terms = (
        jnp.einsum("thkc,thd->hkcd", picked, grad_rounded, preferred_element_type=jnp.float32)
        * inv_scale
    )
    weight_terms = weight_terms.reshape(local_blocks, KSLOT * BLK * BLK)
    weight_grad = lax.psum_scatter(weight_terms, "row", scatter_dimension=1, tiled=True)
    bias_terms = jnp.sum(grad_pre, axis=0).reshape(local_blocks * BLK) * inv_scale
    bias_grad = lax.psum(bias_terms, "row")
    return (activation, weight_grad, bias_grad)


def place(quads):
    row = lax.axis_index("row")
    return row, row // 4, (row // 2) % 2, row % 2, lax.axis_index("col")


def greet(row, quad, bit_y, bit_x, col, quads, extra=()):
    barrier = pltpu.get_barrier_semaphore()
    peers = [(quad * 4 + bit_y * 2 + 1 - bit_x, col), (quad * 4 + (1 - bit_y) * 2 + bit_x, col)]
    peers += [((quad + d) % quads * 4 + bit_y * 2 + bit_x, col) for d in range(1, quads)]
    peers += list(extra)
    for peer in peers:
        pl.semaphore_signal(barrier, inc=1, device_id=peer, device_id_type=MESH)
    pl.semaphore_wait(barrier, len(peers))


def gather_kernel(quads, w_ref, tok_ref, all_ref, peer_ref,
                  own_sem, tok_s, tok_r, z_s, z_r, y_s, y_r, x_s, x_r):
    row, quad, bit_y, bit_x, col = place(quads)
    half = w_ref.shape[0] // 2
    x_peer = (quad * 4 + bit_y * 2 + 1 - bit_x, col)
    y_peer = (quad * 4 + (1 - bit_y) * 2 + bit_x, col)
    greet(row, quad, bit_y, bit_x, col, quads, [(row, 1 - col)])

    def send(src, dst, s, r, peer):
        copy = pltpu.make_async_remote_copy(
            src_ref=src, dst_ref=dst, send_sem=s, recv_sem=r, device_id=peer, device_id_type=MESH
        )
        copy.start()
        return copy

    copies = []
    own = pltpu.make_async_copy(w_ref, all_ref.at[row], own_sem)
    own.start()
    z_copies = {}

    def send_quad(d):
        target = ((quad + d) % quads * 4 + bit_y * 2 + bit_x, col)
        z_copies[d] = send(w_ref, all_ref.at[row], z_s.at[d - 1], z_r.at[d - 1], target)

    order = sorted(range(quads), key=lambda d: min(d, quads - d))
    send_quad(order[1])
    cut = [pl.ds(0, half), pl.ds(half, half)]
    first_y, first_x = {}, {}

    def relay(d):
        from_quad = (quad - d + quads) % quads * 4
        y_row = from_quad + (1 - bit_y) * 2 + bit_x
        x_row = from_quad + bit_y * 2 + 1 - bit_x
        first_y[d].wait_recv()
        piece = all_ref.at[y_row, cut[0]]
        copies.append(send(piece, piece, x_s.at[2 * quads + d], x_r.at[2 * quads + d], x_peer))
        first_x[d].wait_recv()
        piece = all_ref.at[x_row, cut[1]]
        copies.append(send(piece, piece, y_s.at[2 * quads + d], y_r.at[2 * quads + d], y_peer))

    for i, d in enumerate(order):
        src_row = (quad - d + quads) % quads * 4 + bit_y * 2 + bit_x
        if i > 0:
            z_copies[d].wait_recv()
            if i + 1 < quads:
                send_quad(order[i + 1])
        src = [w_ref.at[c] if d == 0 else all_ref.at[src_row, c] for c in cut]
        dst = [all_ref.at[src_row, c] for c in cut]
        first_y[d] = send(src[0], dst[0], y_s.at[d], y_r.at[d], y_peer)
        first_x[d] = send(src[1], dst[1], x_s.at[d], x_r.at[d], x_peer)
        copies.append(send(src[0], dst[0], x_s.at[quads + d], x_r.at[quads + d], x_peer))
        copies.append(send(src[1], dst[1], y_s.at[quads + d], y_r.at[quads + d], y_peer))
        if i == 0:
            tok_copy = send(tok_ref, peer_ref, tok_s, tok_r, (row, 1 - col))
        else:
            relay(order[i - 1])
    relay(order[-1])
    for copy in copies:
        copy.wait()
    for copy in [*z_copies.values(), *first_y.values(), *first_x.values()]:
        copy.wait_send()
    tok_copy.wait()
    own.wait()


def gather(w_flat, tokens, quads):
    any_spec = pl.BlockSpec(memory_space=pl.ANY)
    dma = pltpu.SemaphoreType.DMA
    return pl.pallas_call(
        functools.partial(gather_kernel, quads),
        out_shape=(
            jax.ShapeDtypeStruct((quads * 4,) + w_flat.shape, w_flat.dtype),
            jax.ShapeDtypeStruct(tokens.shape, tokens.dtype),
        ),
        in_specs=[pl.BlockSpec(memory_space=pltpu.VMEM), any_spec],
        out_specs=(any_spec, any_spec),
        scratch_shapes=[dma, dma, dma, dma((quads - 1,)), dma((quads - 1,)),
                        dma((3 * quads,)), dma((3 * quads,)), dma((3 * quads,)), dma((3 * quads,))],
        compiler_params=pltpu.CompilerParams(collective_id=0, has_side_effects=True,
                                             vmem_limit_bytes=VMEM_LIMIT),
    )(w_flat, tokens)


def fused_kernel(quads, chunks, blk_rows, strip, scale,
                 pat_ref, own_ref, peer_ref, w_ref, bias_ref, grad_ref,
                 act_ref, out_ref, bout_ref,
                 table, p_ref, b_ref, first, second, second_out, third, third_out,
                 bx, by, by_out, bz, bz_out,
                 f_s, f_r, s_s, s_r, t_s, t_r, b_s, b_r):
    step = pl.program_id(0)
    steps = pl.num_programs(0)
    rows = quads * 4
    row, quad, bit_y, bit_x, col = place(quads)
    n = first.shape[3]
    half = p_ref.shape[1] // 2
    per = p_ref.shape[1] // chunks // (2 * blk_rows)
    peers = [(quad * 4 + bit_y * 2 + 1 - bit_x, col), (quad * 4 + (1 - bit_y) * 2 + bit_x, col)]

    @pl.when(step == 0)
    def _():
        greet(row, quad, bit_y, bit_x, col, quads)

        panel = own_ref.shape[1] // BLK
        for i in range(panel):
            table[col * panel + i] = own_ref[:, i * BLK:(i + 1) * BLK]
            table[(1 - col) * panel + i] = peer_ref[:, i * BLK:(i + 1) * BLK]

    pair = pair_of(step, per, chunks)
    weights = [w_ref[r].astype(jnp.float32) for r in range(rows)]
    results = []
    for j in range(2):
        piece = pl.ds(j * BLK, BLK)
        w = jnp.concatenate([v[j * blk_rows:(j + 1) * blk_rows] for v in weights], axis=0)
        w = w.astype(jnp.bfloat16)
        base = (2 * pair + j) * KSLOT
        picks = [table[pat_ref[base + k]] for k in range(KSLOT)]
        sel = jnp.concatenate(picks, axis=1)
        v = jnp.dot(sel, w, preferred_element_type=jnp.float32)
        v = v + bias_ref[:, piece].astype(jnp.float32)
        c = math.sqrt(2.0 / math.pi)
        sq = v * v
        t = jnp.tanh(v * (c + (c * 0.044715) * sq))
        lift = 0.5 + 0.5 * t
        act_ref[:, piece] = (v * lift).astype(jnp.bfloat16)
        slope = lift + (0.5 * v) * (1.0 - t * t) * (c + (3.0 * 0.044715 * c) * sq)
        grad = grad_ref[:, piece].astype(jnp.float32) * slope
        b_ref[pl.ds(2 * pair + j, 1), :] = jnp.sum(grad, axis=0, keepdims=True) * scale
        out = lax.dot_general(sel, grad.astype(jnp.bfloat16), (((0,), (0,)), ((), ())),
                              preferred_element_type=jnp.float32)
        results.append(out * scale)
    at = pl.multiple_of(pair * (2 * blk_rows), 2 * blk_rows)
    for r in range(rows):
        cut = slice(r * blk_rows, (r + 1) * blk_rows)
        p_ref[r, pl.ds(at, 2 * blk_rows), :] = jnp.concatenate(
            [o[cut] for o in results], axis=0).astype(p_ref.dtype)

    def link(src, dst, s, r, peer):
        return pltpu.make_async_remote_copy(
            src_ref=src, dst_ref=dst, send_sem=s, recv_sem=r, device_id=peer, device_id_type=MESH
        )

    def piece_row(d, colour, near, far):
        flip_x, flip_y = (near, far) if colour == 0 else (far, near)
        x = (1 - bit_x) if flip_x else bit_x
        y = (1 - bit_y) if flip_y else bit_y
        return (quad + d) % quads * 4 + y * 2 + x

    order = list(range(1, quads)) + [0]
    start = lambda c: (c % 2) * half + (c // 2) * n

    def first_copy(c, far, d):
        return link(p_ref.at[piece_row(d, c % 2, 1, far), pl.ds(start(c), n)],
                    first.at[c, far, d], f_s.at[c, far, d], f_r.at[c, far, d], peers[c % 2])

    def second_copy(c, d):
        return link(second_out.at[c, d], second.at[c, d], s_s.at[c, d], s_r.at[c, d],
                    peers[1 - c % 2])

    def third_copy(c, d):
        target = ((quad + d) % quads * 4 + bit_y * 2 + bit_x, col)
        return link(third_out.at[c, d - 1], third.at[c, d - 1],
                    t_s.at[c, d - 1], t_r.at[c, d - 1], target)

    def do_first(c):
        for far in (1, 0):
            for d in order:
                first_copy(c, far, d).start()

    def do_second(c):
        for d in order:
            first_copy(c, 1, d).wait_recv()
            mine = piece_row(d, c % 2, 0, 1)

            @pl.loop(0, n // strip)
            def _(i, d=d, mine=mine):
                s = pl.multiple_of(i * strip, strip)
                here = p_ref[mine, pl.ds(start(c) + s, strip), :].astype(jnp.float32)
                come = first[c, 1, d, pl.ds(s, strip), :].astype(jnp.float32)
                second_out[c, d, pl.ds(s, strip), :] = (here + come).astype(jnp.bfloat16)

            second_copy(c, d).start()

    def do_third(c):
        for d in order:
            first_copy(c, 0, d).wait_recv()
            second_copy(c, d).wait_recv()
            mine = piece_row(d, c % 2, 0, 0)

            @pl.loop(0, n // strip)
            def _(i, d=d, mine=mine):
                s = pl.multiple_of(i * strip, strip)
                total = p_ref[mine, pl.ds(start(c) + s, strip), :].astype(jnp.float32)
                total += first[c, 0, d, pl.ds(s, strip), :].astype(jnp.float32)
                total += second[c, d, pl.ds(s, strip), :].astype(jnp.float32)
                if d == 0:
                    out_ref[pl.ds(start(c) + s, strip), :] = total
                else:
                    third_out[c, d - 1, pl.ds(s, strip), :] = total.astype(jnp.bfloat16)

            if d > 0:
                third_copy(c, d).start()

    for c in range(chunks):
        @pl.when(step == (c + 1) * per - 1)
        def _(c=c):
            do_first(c)
            if c >= 2:
                do_second(c - 2)
            if c >= 4:
                do_third(c - 4)

    @pl.when(step == steps - 1)
    def _():
        to_x = link(b_ref, bx, b_s.at[0], b_r.at[0], peers[0])
        to_x.start()
        do_second(chunks - 2)
        do_third(chunks - 4)
        to_x.wait()
        by_out[...] = b_ref[...] + bx[...]
        to_y = link(by_out, by, b_s.at[1], b_r.at[1], peers[1])
        to_y.start()
        do_second(chunks - 1)
        do_third(chunks - 3)
        to_y.wait()
        bz_out[...] = by_out[...] + by[...]
        to_z = []
        for d in range(1, quads):
            target = ((quad + d) % quads * 4 + bit_y * 2 + bit_x, col)
            to_z.append(link(bz_out, bz.at[d - 1], b_s.at[d + 1], b_r.at[d + 1], target))
            to_z[-1].start()
        do_third(chunks - 2)
        do_third(chunks - 1)
        for copy in to_z:
            copy.wait()
        total = bz_out[...]
        for d in range(quads - 1):
            total += bz[d]
        bout_ref[...] = total
        for c in range(chunks):
            for d in range(1, quads):
                third_copy(c, d).wait()

            @pl.loop(0, n // strip)
            def _(i, c=c):
                s = pl.multiple_of(i * strip, strip)
                total = out_ref[pl.ds(start(c) + s, strip), :]
                for d in range(quads - 1):
                    total += third[c, d, pl.ds(s, strip), :].astype(jnp.float32)
                out_ref[pl.ds(start(c) + s, strip), :] = total
        for c in range(chunks):
            for d in order:
                first_copy(c, 0, d).wait_send()
                first_copy(c, 1, d).wait_send()
                second_copy(c, d).wait_send()


def pair_of(step, per, chunks):
    chunk = step // per
    return (chunk % 2) * (per * chunks // 2) + (chunk // 2) * per + step % per


def fused(pat, own, peer, weights, bias, grad_act, quads, scale):
    tok, hidden = grad_act.shape
    blocks = hidden // BLK
    steps = blocks // 2
    total_rows = weights.shape[1]
    chunks = 8 if steps % 8 == 0 and total_rows % 128 == 0 else 4
    per = steps // chunks
    blk_rows = total_rows // blocks
    n = total_rows // chunks
    strip = next(c for c in (240, 160, 128, 96, 80, 64, 48, 32, 16) if n % c == 0)
    rows = quads * 4
    whole = lambda a: pl.BlockSpec(a.shape, lambda i, p: (0, 0))
    wide = lambda m: pl.BlockSpec((m, 2 * BLK), lambda i, p: (0, pair_of(i, per, chunks)))
    fixed = lambda *s: pl.BlockSpec(s, lambda i, p: (0, 0))
    cube = pl.BlockSpec((rows, 2 * blk_rows, BLK), lambda i, p: (0, pair_of(i, per, chunks), 0))
    dma = pltpu.SemaphoreType.DMA
    bf = lambda *s: pltpu.VMEM(s, jnp.bfloat16)
    f32 = lambda *s: pltpu.VMEM(s, jnp.float32)
    b = (blocks, BLK)
    return pl.pallas_call(
        functools.partial(fused_kernel, quads, chunks, blk_rows, strip, scale),
        out_shape=(
            jax.ShapeDtypeStruct((tok, hidden), jnp.bfloat16),
            jax.ShapeDtypeStruct((total_rows, BLK), jnp.float32),
            jax.ShapeDtypeStruct(b, jnp.float32),
        ),
        grid_spec=pltpu.PrefetchScalarGridSpec(
            num_scalar_prefetch=1, grid=(steps,),
            in_specs=[whole(own), whole(peer), cube, wide(1), wide(tok)],
            out_specs=[wide(tok), fixed(total_rows, BLK), fixed(*b)],
            scratch_shapes=[
                bf(2 * own.shape[1] // BLK, tok, BLK), bf(rows, total_rows, BLK), f32(*b),
                bf(chunks, 2, quads, n, BLK), bf(chunks, quads, n, BLK), bf(chunks, quads, n, BLK),
                bf(chunks, quads - 1, n, BLK), bf(chunks, quads - 1, n, BLK),
                f32(*b), f32(*b), f32(*b), f32(quads - 1, *b), f32(*b),
                dma((chunks, 2, quads)), dma((chunks, 2, quads)), dma((chunks, quads)),
                dma((chunks, quads)), dma((chunks, quads - 1)), dma((chunks, quads - 1)),
                dma((quads + 1,)), dma((quads + 1,)),
            ],
        ),
        compiler_params=pltpu.CompilerParams(collective_id=1, has_side_effects=True,
                                             vmem_limit_bytes=VMEM_LIMIT),
    )(pat, own, peer, weights, bias, grad_act)


def kernel_body(tokens, w_blocks, hidden_bias, pattern, grad_act):
    tok_rows = tokens.shape[0]
    local_blocks, width = w_blocks.shape
    rows = lax.axis_size("row")
    quads = rows // 4
    col = lax.axis_index("col")
    scale = 1.0 / math.sqrt(tok_rows * rows)
    pat = lax.dynamic_slice_in_dim(pattern, col * local_blocks, local_blocks, 0).reshape(-1)
    flat = w_blocks.reshape(local_blocks * width // BLK, BLK)
    weights, peer = gather(flat, tokens, quads)
    activation, weight_grad, bias_grad = fused(
        pat, tokens, peer, weights, hidden_bias.reshape(1, -1), grad_act, quads, scale)
    return activation, weight_grad.reshape(local_blocks, width), bias_grad.reshape(-1)


def body(tokens, w_blocks, hidden_bias, pattern, grad_act):
    rows = lax.axis_size("row")
    piece = w_blocks.shape[1] // BLK
    fits = lax.axis_size("col") == 2 and rows % 4 == 0 and rows > 4
    fits = fits and piece % 8 == 0 and w_blocks.shape[0] % 8 == 0
    run = kernel_body if fits else plain_body
    return run(tokens, w_blocks, hidden_bias, pattern, grad_act)


def solution(mesh):
    return jax.shard_map(
        body,
        mesh=mesh,
        in_specs=(P("row", "col"), P("col", "row"), P("col"), P(), P("row", "col")),
        out_specs=(P("row", "col"), P("col", "row"), P("col")),
        check_vma=False,
    )
```
